512 devices in a mesh: grp: 64 (over z, y), row: 8 (over x, core).
Axes of the slice: x: 4, y: 8, z: 8, core: 2. Of those that a mesh axis runs over, the one named last changes fastest.
Arguments:
- latents: bfloat16 [64, 16384], P('grp'), may hold values from -6 to 6
- frames: int32 [64], replicated, may hold values from 1 to 4, as said below
- offsets: int32 [64], replicated, may hold values from 0 to 1008, as said below
- assign: int32 [64], replicated, may hold values from 0 to 63, each once
- w_in: bfloat16 [16, 27, 384], replicated, may hold values from -0.3125 to 0.3125
- w_mid: bfloat16 [384, 27, 192], P('grp'), may hold values from -0.0625 to 0.0625
- w_out: bfloat16 [192, 27, 96], P('grp'), may hold values from -0.078125 to 0.078125
- gain_in: float32 [384], replicated, may hold values from 0.25 to 1.75
- gain_mid: float32 [192], replicated, may hold values from 0.25 to 1.75
- gain_out: float32 [96], replicated, may hold values from 0.25 to 1.75
Outputs:
- decoded: bfloat16 [64, 4, 64, 6144], P('grp', None, 'row')
The draws below stay inside these ranges and needn't reach their ends.
Inputs may be any that keep to these rules, and one draw needn't show every extreme that they name: Some request has exactly 4 frames. The blocks of different requests do not intersect, and offsets[r] + 16 <= 1024 for every request; some request starts at 1008. `assign`: every request is decoded by exactly one group.
All inputs are finite; a program needn't handle non-finite values.
Results may differ from the reference program's by a relative error of at most 0.006.
Values may be sent and summed in bfloat16 or wider, within the bound.
A program may use at most 128 MiB of HBM per device.

```python
import jax
import jax.numpy as jnp
from jax import lax

ZC = 16
C1 = 384
C2 = 192
C3 = 96
WL = 16
FMAX = 4
HL = 16
REQS = 64
SPAN = 4
CAP = 16
BUF = 1024
N_GRP = 64


def shared_plan(key):
    plan_key = jax.random.fold_in(key, 11)
    key_base, key_large, key_order = jax.random.split(plan_key, 3)
    base = jax.random.randint(key_base, (REQS,), 1, min(FMAX // 2 + 1, FMAX) + 1, dtype=jnp.int32)
    largest = jax.random.randint(key_large, (), 0, REQS, dtype=jnp.int32)
    counts = jnp.where(jnp.arange(REQS, dtype=jnp.int32) == largest, FMAX, base).astype(jnp.int32)
    order = jax.random.permutation(key_order, REQS)
    lengths = counts[order] * SPAN
    starts = (jnp.cumsum(lengths) - lengths).astype(jnp.int32)
    last = jnp.arange(REQS, dtype=jnp.int32) == REQS - 1
    starts = jnp.where(last, BUF - CAP, starts).astype(jnp.int32)
    placed = jnp.zeros((REQS,), jnp.int32).at[order].set(starts)
    return (counts, placed)


def draw_frames(key, part):
    return shared_plan(key)[0]


def draw_offsets(key, part):
    return shared_plan(key)[1]


def block_levels(key, shape, pieces, smallest, high):
    factor_of, own = 1.0, jax.random.fold_in(key, 6)
    for axis_at, blocks in pieces:
        heights = jnp.exp(jax.random.uniform(jax.random.fold_in(own, axis_at), (blocks,), jnp.float32, smallest / len(pieces), high / len(pieces)))
        factor_of = factor_of * jnp.repeat(heights, shape[axis_at] // blocks).reshape([-1 if axis == axis_at else 1 for axis in range(len(shape))])
    return factor_of


def bell_draw(rng, extent, spread, limit, pieces=(), held_as=jnp.bfloat16):
    loudness = block_levels(rng, extent, pieces, -0.22, 0.18) if pieces else 1.0
    drawn = jax.random.normal(rng, extent, jnp.float32) * spread * loudness
    return jnp.minimum(jnp.maximum(drawn, -limit), limit).astype(held_as)


def setup_inputs(seed: int = 0) -> dict:
    seeds = jax.random.split(jax.random.key(seed), 11)
    return {
        "latents": bell_draw(seeds[0], (N_GRP, BUF * ZC), 1.0, 6.0, ((0, 64),)),
        "frames": draw_frames(jax.random.fold_in(seeds[10], 71), 0),
        "offsets": draw_offsets(jax.random.fold_in(seeds[10], 71), 0),
        "assign": jax.random.permutation(seeds[3], REQS).astype(jnp.int32),
        "w_in": bell_draw(seeds[4], (ZC, 27, C1), (27 * ZC) ** -0.5, 0.3125),
        "w_mid": bell_draw(seeds[5], (C1, 27, C2), (27 * C1) ** -0.5, 0.0625, ((0, 64),)),
        "w_out": bell_draw(seeds[6], (C2, 27, C3), (27 * C2) ** -0.5, 0.078125, ((0, 64),)),
        "gain_in": jnp.clip(1.0 + 0.15 * jax.random.normal(seeds[7], (C1,), jnp.float32), 0.25, 1.75),
        "gain_mid": jnp.clip(1.0 + 0.15 * jax.random.normal(seeds[8], (C2,), jnp.float32), 0.25, 1.75),
        "gain_out": jnp.clip(1.0 + 0.15 * jax.random.normal(seeds[9], (C3,), jnp.float32), 0.25, 1.75),
    }


def rms_silu(hidden, gain):
    mean_sq = lax.optimization_barrier(jnp.mean(hidden * hidden, axis=-1, keepdims=True))
    scaled = hidden * lax.rsqrt(mean_sq + 1e-06) * gain
    return jax.nn.silu(scaled)

def causal_conv(extended, weight):
    count_t = extended.shape[0]
    count_r = extended.shape[1] - 2
    count_c = extended.shape[2]
    width_in = extended.shape[3]
    width_out = weight.shape[2]
    padded = jnp.pad(extended, ((2, 0), (0, 0), (1, 1), (0, 0)))
    total = jnp.zeros((count_t * count_r * count_c, width_out), jnp.float32)
    for time_tap in range(3):
        for row_tap in range(3):
            for col_tap in range(3):
                window = padded[time_tap:time_tap + count_t, row_tap:row_tap + count_r, col_tap:col_tap + count_c]
                window = window.reshape(count_t * count_r * count_c, width_in)
                tap_index = 9 * time_tap + 3 * row_tap + col_tap
                total = total + jnp.dot(window, weight[:, tap_index, :], preferred_element_type=jnp.float32)
    return total.reshape(count_t, count_r, count_c, width_out)

def upsample(values):
    return jnp.repeat(jnp.repeat(values, 2, axis=1), 2, axis=2)

def pad_rows(values):
    return jnp.pad(values, ((0, 0), (1, 1), (0, 0), (0, 0)))

def reference(latents, frames, offsets, assign, w_in, w_mid, w_out, gain_in, gain_mid, gain_out):
    table = latents.reshape(N_GRP, BUF, ZC)
    frame_ids = jnp.arange(FMAX, dtype=jnp.int32)[:, None, None]
    row_ids = jnp.arange(HL, dtype=jnp.int32)[None, :, None]
    col_ids = jnp.arange(WL, dtype=jnp.int32)[None, None, :]
    position = (frame_ids * HL + row_ids) * WL + col_ids

    def decode(group):
        request = assign[group]
        count = frames[request]
        fill_len = count * SPAN
        shard = jnp.minimum(position // fill_len, N_GRP - 1).astype(jnp.int32)
        within = (position % fill_len).astype(jnp.int32)
        tokens = table[shard, offsets[request] + within]
        valid = (frame_ids < count)[..., None]
        latent_in = jnp.where(valid, tokens, jnp.zeros((), jnp.bfloat16)).astype(jnp.bfloat16)
        act_in = rms_silu(causal_conv(pad_rows(latent_in), w_in), gain_in).astype(jnp.bfloat16)
        act_mid = rms_silu(causal_conv(pad_rows(upsample(act_in)), w_mid), gain_mid).astype(jnp.bfloat16)
        final = rms_silu(causal_conv(pad_rows(upsample(act_mid)), w_out), gain_out)
        final = jnp.where(valid, final, jnp.zeros((), jnp.float32))
        return final.astype(jnp.bfloat16).reshape(FMAX, 4 * HL, 4 * WL * C3)
    return lax.map(decode, jnp.arange(N_GRP, dtype=jnp.int32))
```

```python
import jax
import jax.numpy as jnp
from jax import lax
from jax.experimental import pallas as pl
from jax.experimental.pallas import tpu as pltpu
from jax.sharding import PartitionSpec as P

RL = 2
WL = 16
FMAX = 4
C1 = 384
C2 = 192
C3 = 96
C1P = 512
NB = 1792
EPS = 1e-06
F32 = jnp.float32
BF16 = jnp.bfloat16


def silu_norm(h, gain, width):
    mean_sq = jnp.sum(h * h, axis=-1, keepdims=True) * (1.0 / width)
    v = h * lax.rsqrt(mean_sq + EPS) * gain
    return v / (1.0 + jnp.exp(-v))


def iota(shape, dim):
    return lax.broadcasted_iota(jnp.int32, shape, dim)


def decode_kernel(
    info, xt_ref, win_ref, wmid_ref, wout_ref, gin_ref, gmid_ref, gout_ref, o_ref,
    cols, act1, z1, act2, z2, flat,
):
    row = info[0]
    count = info[1]

    xt = xt_ref[...].astype(F32)
    lane = iota(xt.shape, 1) % WL
    shifted = (
        jnp.where(lane == WL - 1, 0.0, xt),
        xt,
        jnp.where(lane == 0, 0.0, xt),
    )
    width = xt.shape[1]
    for a in range(3):
        for b in range(3):
            for e in range(3):
                start = 320 + (a - 2) * 96 + (b - 1) * 16 + (e - 1)
                piece = pltpu.roll(shifted[e], width - start, 1)[:, :384]
                k = 9 * a + 3 * b + e
                cols[16 * k : 16 * k + 16, :] = piece.astype(BF16)
    h = lax.dot_general(
        cols[...], win_ref[...], (((0,), (0,)), ((), ())), preferred_element_type=F32
    )
    act = silu_norm(h, gin_ref[...], C1).astype(BF16)
    src = iota((C1, C1P), 0)
    dst = iota((C1, C1P), 1)
    place = ((dst // 8 * 6 + dst % 8 == src) & (dst % 8 < 6)).astype(F32).astype(BF16)
    spread = jnp.dot(act, place, preferred_element_type=F32)
    act1[0:128, :] = jnp.zeros((128, C1P), BF16)
    rid = 2 * row - 1 + iota((64, 1), 0) // WL
    keep = (rid >= 0) & (rid < 16)
    for t in range(FMAX):
        part = spread[t * 96 + 16 : t * 96 + 80, :]
        act1[128 + 64 * t : 192 + 64 * t, :] = jnp.where(keep, part, 0.0).astype(BF16)

    for a in range(3):
        part = jnp.dot(
            act1[64 * a : 64 * a + 256, :],
            wmid_ref[:, NB * a : NB * a + NB],
            preferred_element_type=F32,
        )
        if a == 0:
            z1[...] = part
        else:
            z1[...] += part

    act2[0:384, :] = jnp.zeros((384, C2), BF16)
    xpos = iota((64, 1), 0) % WL
    gmid = gmid_ref[...]
    for t in range(FMAX):
        combos = []
        for b in range(3):
            z = []
            for e in range(3):
                k = 3 * b + e
                if k % 2 == 0:
                    z.append(z1[64 * t : 64 * t + 64, 192 * k : 192 * k + 192])
                else:
                    win = z1[64 * t : 64 * t + 64, 192 * k - 64 : 192 * k + 192]
                    z.append(pltpu.roll(win, 192, 1)[:, :192])
            left = jnp.where(xpos == 0, 0.0, pltpu.roll(z[0], 1, 0))
            right = jnp.where(xpos == WL - 1, 0.0, pltpu.roll(z[2], 63, 0))
            combos.append((left + z[1] + z[2], z[0] + z[1] + right))
        for m in range(6):
            y, p = (m + 1) // 2, (m + 1) % 2
            rows = (y, y, y + 1) if p else (y - 1, y, y)
            rid2 = 4 * row - 1 + m
            ok = (rid2 >= 0) & (rid2 < 32)
            for q in range(2):
                h = sum(combos[b][q][16 * rows[b] : 16 * rows[b] + 16, :] for b in range(3))
                v = jnp.where(ok, silu_norm(h, gmid, C2), 0.0)
                at = ((t + 2) * 12 + m * 2 + q) * 16
                act2[at : at + 16, :] = v.astype(BF16)

    for a in range(3):
        part = jnp.dot(
            act2[192 * a : 192 * a + 768, :], wout_ref[a], preferred_element_type=F32
        )
        if a == 0:
            z2[...] = part
        else:
            z2[...] += part

    xpos = iota((96, 1), 0) % WL
    gout = gout_ref[...]
    lanes = iota((64, 128), 1)
    for t in range(FMAX):
        combos = []
        for b in range(3):
            z = []
            for e in range(3):
                k = 3 * b + e
                block = z2[192 * t : 192 * t + 192, 128 * k : 128 * k + 128].reshape(6, 2, 16, 128)
                z.append((block[:, 0].reshape(96, 128), block[:, 1].reshape(96, 128)))
            left = (jnp.where(xpos == 0, 0.0, pltpu.roll(z[0][1], 1, 0)), z[0][0])
            right = (z[2][1], jnp.where(xpos == WL - 1, 0.0, pltpu.roll(z[2][0], 95, 0)))
            combos.append(
                [
                    (left[q] + z[1][q] + z[2][q], z[0][q] + z[1][q] + right[q])
                    for q in range(2)
                ]
            )
        for p in range(2):
            phases = []
            for q in range(2):
                for q2 in range(2):
                    c = [combos[b][q][q2] for b in range(3)]
                    if p:
                        h = c[0][16:80] + c[1][16:80] + c[2][32:96]
                    else:
                        h = c[0][0:64] + c[1][16:80] + c[2][16:80]
                    phases.append(jnp.where(t < count, silu_norm(h, gout, C3), 0.0))
            r1 = pltpu.roll(phases[1], 96, 1)
            r2 = pltpu.roll(phases[2], 64, 1)
            r3 = pltpu.roll(phases[3], 32, 1)
            tiles = (
                jnp.where(lanes < 96, phases[0], r1),
                jnp.where(lanes < 64, r1, r2),
                jnp.where(lanes < 32, r2, r3),
            )
            for m in range(4):
                at = (t * 8 + 2 * m + p) * 16
                for j in range(3):
                    flat[j, at : at + 16, :] = tiles[j][16 * m : 16 * m + 16]
        for x in range(WL):
            for j in range(3):
                v = flat[j, pl.ds(t * 128 + x, 8, stride=16), :]
                at = x * 384 + j * 128
                o_ref[0, t, :, at : at + 128] = v.astype(BF16)


def decode(info, xt, win, wmid, wout, gin, gmid, gout):
    vm = pl.BlockSpec(memory_space=pltpu.VMEM)
    return pl.pallas_call(
        decode_kernel,
        name="decode",
        out_shape=jax.ShapeDtypeStruct((1, FMAX, 4 * RL, 4 * WL * C3), BF16),
        in_specs=[pl.BlockSpec(memory_space=pltpu.SMEM)] + [vm] * 7,
        out_specs=vm,
        scratch_shapes=[
            pltpu.VMEM((432, 384), BF16),
            pltpu.VMEM((384, C1P), BF16),
            pltpu.VMEM((256, NB), F32),
            pltpu.VMEM((1152, C2), BF16),
            pltpu.VMEM((768, 1152), F32),
            pltpu.VMEM((3, 512, 128), F32),
        ],
        compiler_params=pltpu.CompilerParams(vmem_limit_bytes=48 * 1024 * 1024),
    )(info, xt, win, wmid, wout, gin, gmid, gout)


def per_device(latents, frames, offsets, assign, w_in, w_mid, w_out, gain_in, gain_mid, gain_out):
    groups = lax.axis_size("grp")
    row_index = lax.axis_index("row")
    group_index = lax.axis_index("grp")
    channels = w_in.shape[0]
    cap_vals = latents.shape[1] // groups
    cap_tokens = cap_vals // channels
    span_len = cap_tokens // FMAX

    mid = w_mid.reshape(6, 3, 9 * C2)
    mid = jnp.pad(mid, ((0, 2), (0, 0), (0, NB - 9 * C2))).reshape(8, 3 * NB)
    full_mid = lax.all_gather(mid, "grp", axis=0, tiled=True)
    full_out = lax.all_gather(w_out, "grp", axis=0, tiled=True)
    wout = jnp.pad(full_out, ((0, 0), (0, 0), (0, 128 - C3)))
    wout = wout.reshape(C2, 3, 9 * 128).transpose(1, 0, 2)
    win = w_in.transpose(1, 0, 2).reshape(27 * channels, C1)

    table = latents.reshape(128, 128)
    start = offsets[assign]
    length = frames[assign] * (span_len * channels)
    first = start // 8
    want = first[:, None] + jnp.arange(3, dtype=jnp.int32)[None, :]
    pick = (want.reshape(-1)[:, None] == jnp.arange(128, dtype=jnp.int32)[None, :]).astype(BF16)
    rows = jnp.dot(pick, table, preferred_element_type=F32).astype(BF16).reshape(groups, 384)
    shift = (start % 8)[:, None]
    for bit in (4, 2, 1):
        moved = jnp.pad(rows[:, 16 * bit :], ((0, 0), (0, 16 * bit)))
        rows = jnp.where((shift & bit) != 0, moved, rows)
    keep = jnp.arange(cap_vals, dtype=jnp.int32)[None, :] < length[:, None]
    outgoing = jnp.where(keep, rows[:, :cap_vals], jnp.zeros((), BF16))
    incoming = lax.all_to_all(outgoing, "grp", split_axis=0, concat_axis=0, tiled=True)

    tokens = incoming.reshape(groups * cap_tokens, channels)
    request = assign[group_index]
    count = frames[request]
    fill_len = count * span_len
    frame_ids = jnp.arange(FMAX, dtype=jnp.int32)[:, None, None]
    row_ids = row_index * RL - 2 + jnp.arange(6, dtype=jnp.int32)[None, :, None]
    col_ids = jnp.arange(WL, dtype=jnp.int32)[None, None, :]
    position = (frame_ids * 16 + row_ids) * WL + col_ids
    valid = (row_ids >= 0) & (row_ids < 16) & (frame_ids < count) & (col_ids >= 0)
    position = jnp.where(valid, position, 0)
    shard = jnp.minimum(position // fill_len, groups - 1)
    within = position % fill_len
    picked = tokens[(shard * cap_tokens + within).reshape(-1)]
    picked = jnp.where(valid.reshape(-1, 1), picked, jnp.zeros((), BF16))
    xt = jnp.pad(picked.T, ((0, 0), (320, 64)))
    info = jnp.stack([row_index.astype(jnp.int32), count])
    gout = jnp.pad(gain_out, (0, 128 - C3)).reshape(1, 128)
    return decode(
        info, xt, win, full_mid, wout, gain_in.reshape(1, C1), gain_mid.reshape(1, C2), gout
    )


def solution(mesh):
    placed = (
        P("grp", None),
        P(),
        P(),
        P(),
        P(),
        P("grp", None, None),
        P("grp", None, None),
        P(),
        P(),
        P(),
    )
    return jax.shard_map(
        per_device,
        mesh=mesh,
        in_specs=placed,
        out_specs=P("grp", None, "row", None),
        check_vma=False,
    )
```

```python
import jax
import jax.numpy as jnp
from jax import lax
from jax.experimental import pallas as pl
from jax.experimental.pallas import tpu as pltpu
from jax.sharding import PartitionSpec as P

RL = 2
WL = 16
FMAX = 4
C1 = 384
C2 = 192
C3 = 96
C1P = 512
NB = 1792
MIDH = 3 * NB // 2
HALF = MIDH + 9 * 128
MID_PARTS = (
    (0, 0, 0, 0, NB),
    (1, 0, NB, 0, NB // 2),
    (1, 1, 0, NB // 2, NB // 2),
    (2, 1, NB // 2, 0, NB),
)
EPS = 1e-06
F32 = jnp.float32
BF16 = jnp.bfloat16
MESH = pl.DeviceIdType.MESH


def silu_norm(h, gain, width):
    mean_sq = jnp.sum(h * h, axis=-1, keepdims=True) * (1.0 / width)
    v = h * lax.rsqrt(mean_sq + EPS) * gain
    return v / (1.0 + jnp.exp(-v))


def iota(shape, dim):
    return lax.broadcasted_iota(jnp.int32, shape, dim)


def decode_kernel(
    info, xt_ref, win_ref, w_ref, gin_ref, gmid_ref, gout_ref, o_ref,
    cols, act1, z1, act2, lhs, z2, flat,
):
    row = info[0]
    count = info[1]

    xt = xt_ref[...].astype(F32)
    lane = iota(xt.shape, 1) % WL
    shifted = (
        jnp.where(lane == WL - 1, 0.0, xt),
        xt,
        jnp.where(lane == 0, 0.0, xt),
    )
    width = xt.shape[1]
    for a in range(3):
        for b in range(3):
            for e in range(3):
                start = 320 + (a - 2) * 96 + (b - 1) * 16 + (e - 1)
                piece = pltpu.roll(shifted[e], width - start, 1)[:, :384]
                k = 9 * a + 3 * b + e
                cols[16 * k : 16 * k + 16, :] = piece.astype(BF16)
    h = lax.dot_general(
        cols[...], win_ref[...], (((0,), (0,)), ((), ())), preferred_element_type=F32
    )
    act = silu_norm(h, gin_ref[...], C1).astype(BF16)
    src = iota((C1, C1P), 0)
    dst = iota((C1, C1P), 1)
    place = ((dst // 8 * 6 + dst % 8 == src) & (dst % 8 < 6)).astype(F32).astype(BF16)
    spread = jnp.dot(act, place, preferred_element_type=F32)
    act1[0:128, :] = jnp.zeros((128, C1P), BF16)
    rid = 2 * row - 1 + iota((64, 1), 0) // WL
    keep = (rid >= 0) & (rid < 16)
    for t in range(FMAX):
        part = spread[t * 96 + 16 : t * 96 + 80, :]
        act1[128 + 64 * t : 192 + 64 * t, :] = jnp.where(keep, part, 0.0).astype(BF16)

    for a, half, start, at, size in MID_PARTS:
        part = jnp.dot(
            act1[64 * a : 64 * a + 256, :],
            w_ref[half, :, start : start + size],
            preferred_element_type=F32,
        )
        if a == 0:
            z1[:, at : at + size] = part
        else:
            z1[:, at : at + size] += part

    act2[0:384, :] = jnp.zeros((384, C2), BF16)
    xpos = iota((64, 1), 0) % WL
    gmid = gmid_ref[...]
    for t in range(FMAX):
        combos = []
        for b in range(3):
            z = []
            for e in range(3):
                k = 3 * b + e
                if k % 2 == 0:
                    z.append(z1[64 * t : 64 * t + 64, 192 * k : 192 * k + 192])
                else:
                    win = z1[64 * t : 64 * t + 64, 192 * k - 64 : 192 * k + 192]
                    z.append(pltpu.roll(win, 192, 1)[:, :192])
            left = jnp.where(xpos == 0, 0.0, pltpu.roll(z[0], 1, 0))
            right = jnp.where(xpos == WL - 1, 0.0, pltpu.roll(z[2], 63, 0))
            combos.append((left + z[1] + z[2], z[0] + z[1] + right))
        for m in range(6):
            y, p = (m + 1) // 2, (m + 1) % 2
            rows = (y, y, y + 1) if p else (y - 1, y, y)
            rid2 = 4 * row - 1 + m
            ok = (rid2 >= 0) & (rid2 < 32)
            for q in range(2):
                h = sum(combos[b][q][16 * rows[b] : 16 * rows[b] + 16, :] for b in range(3))
                v = jnp.where(ok, silu_norm(h, gmid, C2), 0.0)
                at = ((t + 2) * 12 + m * 2 + q) * 16
                act2[at : at + 16, :] = v.astype(BF16)

    src = iota((C2, 512), 0)
    dst = iota((C2, 512), 1)
    low = ((dst // 8 * 3 + dst % 8 == src) & (dst % 8 < 3)).astype(F32).astype(BF16)
    high = ((dst // 8 * 3 + dst % 8 - 4 == src) & (dst % 8 >= 4) & (dst % 8 < 7)).astype(F32)
    high = high.astype(BF16)
    both = jnp.dot(act2[0:768, :], low, preferred_element_type=F32)
    both += jnp.dot(act2[192:960, :], high, preferred_element_type=F32)
    lhs[0] = both.astype(BF16)
    lhs[1] = jnp.dot(act2[384:1152, :], low, preferred_element_type=F32).astype(BF16)
    z2[...] = jnp.dot(lhs[0], w_ref[0, :, MIDH:HALF], preferred_element_type=F32)
    z2[...] += jnp.dot(lhs[1], w_ref[1, :, MIDH:HALF], preferred_element_type=F32)

    xpos = iota((96, 1), 0) % WL
    gout = gout_ref[...]
    lanes = iota((64, 128), 1)
    for t in range(FMAX):
        combos = []
        for b in range(3):
            z = []
            for e in range(3):
                k = 3 * b + e
                block = z2[192 * t : 192 * t + 192, 128 * k : 128 * k + 128].reshape(6, 2, 16, 128)
                z.append((block[:, 0].reshape(96, 128), block[:, 1].reshape(96, 128)))
            left = (jnp.where(xpos == 0, 0.0, pltpu.roll(z[0][1], 1, 0)), z[0][0])
            right = (z[2][1], jnp.where(xpos == WL - 1, 0.0, pltpu.roll(z[2][0], 95, 0)))
            combos.append(
                [
                    (left[q] + z[1][q] + z[2][q], z[0][q] + z[1][q] + right[q])
                    for q in range(2)
                ]
            )
        for p in range(2):
            phases = []
            for q in range(2):
                for q2 in range(2):
                    c = [combos[b][q][q2] for b in range(3)]
                    if p:
                        h = c[0][16:80] + c[1][16:80] + c[2][32:96]
                    else:
                        h = c[0][0:64] + c[1][16:80] + c[2][16:80]
                    phases.append(jnp.where(t < count, silu_norm(h, gout, C3), 0.0))
            r1 = pltpu.roll(phases[1], 96, 1)
            r2 = pltpu.roll(phases[2], 64, 1)
            r3 = pltpu.roll(phases[3], 32, 1)
            tiles = (
                jnp.where(lanes < 96, phases[0], r1),
                jnp.where(lanes < 64, r1, r2),
                jnp.where(lanes < 32, r2, r3),
            )
            for m in range(4):
                at = (t * 8 + 2 * m + p) * 16
                for j in range(3):
                    flat[j, at : at + 16, :] = tiles[j][16 * m : 16 * m + 16]
        for x in range(WL):
            for j in range(3):
                v = flat[j, pl.ds(t * 128 + x, 8, stride=16), :]
                at = x * 384 + j * 128
                o_ref[0, t, :, at : at + 128] = v.astype(BF16)


def decode(info, xt, win, weights, gin, gmid, gout):
    vm = pl.BlockSpec(memory_space=pltpu.VMEM)
    return pl.pallas_call(
        decode_kernel,
        name="decode",
        out_shape=jax.ShapeDtypeStruct((1, FMAX, 4 * RL, 4 * WL * C3), BF16),
        in_specs=[pl.BlockSpec(memory_space=pltpu.SMEM)] + [vm] * 6,
        out_specs=vm,
        scratch_shapes=[
            pltpu.VMEM((432, 384), BF16),
            pltpu.VMEM((384, C1P), BF16),
            pltpu.VMEM((256, NB), F32),
            pltpu.VMEM((1152, C2), BF16),
            pltpu.VMEM((2, 768, 512), BF16),
            pltpu.VMEM((768, 1152), F32),
            pltpu.VMEM((3, 512, 128), F32),
        ],
        compiler_params=pltpu.CompilerParams(vmem_limit_bytes=56 * 1024 * 1024),
    )(info, xt, win, weights, gin, gmid, gout)


def gather_kernel(x_ref, g_ref, own_sem, send_sem, recv_sem):
    grp = lax.axis_index("grp")
    row = lax.axis_index("row")
    core = row % 2
    step1 = 1 + 7 * core
    step2 = 8 - 7 * core
    i1 = (grp // step1) % 8
    i2 = (grp // step2) % 8

    def slot(a, b):
        return (a % 8) * step1 + (b % 8) * step2

    right1, left1 = (slot(i1 + 1, i2), row), (slot(i1 + 7, i2), row)
    right2, left2 = (slot(i1, i2 + 1), row), (slot(i1, i2 + 7), row)
    partner = (grp, row + 1 - 2 * core)

    barrier = pltpu.get_barrier_semaphore()
    for peer in (right1, left1, right2, left2, partner):
        pl.semaphore_signal(barrier, inc=1, device_id=peer, device_id_type=MESH)
    pl.semaphore_wait(barrier, 5)

    started = []

    def send(way, peer, a, b, own=False):
        at = slot(a, b)
        copy = pltpu.make_async_remote_copy(
            src_ref=x_ref.at[core] if own else g_ref.at[core, at],
            dst_ref=g_ref.at[core, at],
            send_sem=send_sem.at[way, at],
            recv_sem=recv_sem.at[core, at],
            device_id=peer,
            device_id_type=MESH,
        )
        copy.start()
        started.append(copy)

    def arrived(half, at):
        pltpu.make_async_remote_copy(
            src_ref=g_ref.at[half, at],
            dst_ref=g_ref.at[half, at],
            send_sem=send_sem.at[0, at],
            recv_sem=recv_sem.at[half, at],
            device_id=partner,
            device_id_type=MESH,
        ).wait_recv()

    send(0, right1, i1, i2, True)
    send(1, left1, i1, i2, True)
    send(2, right2, i1, i2, True)
    send(3, left2, i1, i2, True)
    local = [
        pltpu.make_async_copy(x_ref.at[h], g_ref.at[h, grp], own_sem.at[h]) for h in range(2)
    ]
    for copy in local:
        copy.start()

    line = [0, -1, 1, -2, 2, -3, 3, -4]
    for off in line[1:]:
        arrived(core, slot(i1 + off + 8, i2))
        if -4 < off < 0:
            send(0, right1, i1 + off + 8, i2)
        if 0 < off < 3:
            send(1, left1, i1 + off + 8, i2)
        send(2, right2, i1 + off + 8, i2)
        send(3, left2, i1 + off + 8, i2)
        send(4, partner, i1 + off + 8, i2)

    for dist in range(1, 5):
        for n, off in enumerate(line):
            a = i1 + off + 8
            for sign in (-1, 1):
                if dist == 4 and (n % 2 == 0) != (sign < 0):
                    continue
                b = i2 + sign * dist + 8
                arrived(core, slot(a, b))
                if dist < 3 or (dist == 3 and (n % 2 == 0) == (sign < 0)):
                    send(2 if sign < 0 else 3, right2 if sign < 0 else left2, a, b)
                send(4, partner, a, b)

    for n in range(1, 64):
        arrived(1 - core, (grp + n) % 64)
    for copy in started:
        copy.wait_send()
    for copy in local:
        copy.wait()


def gather_weights(x):
    any_spec = pl.BlockSpec(memory_space=pl.ANY)
    return pl.pallas_call(
        gather_kernel,
        name="gather",
        out_shape=jax.ShapeDtypeStruct((2, 64, 8, HALF), BF16),
        in_specs=[any_spec],
        out_specs=any_spec,
        scratch_shapes=[
            pltpu.SemaphoreType.DMA((2,)),
            pltpu.SemaphoreType.DMA((5, 64)),
            pltpu.SemaphoreType.DMA((2, 64)),
        ],
        compiler_params=pltpu.CompilerParams(collective_id=0, has_side_effects=True),
    )(x)


def pack_weights(w_mid, w_out):
    mid = w_mid.reshape(6, 3, 9 * C2)
    mid = jnp.pad(mid, ((0, 2), (0, 0), (0, NB - 9 * C2))).reshape(8, 3 * NB)
    out = jnp.pad(w_out, ((0, 0), (0, 0), (0, 128 - C3))).reshape(3, 3, 9 * 128)
    out = jnp.pad(out.transpose(1, 0, 2), ((0, 1), (0, 1), (0, 0))).reshape(2, 8, 9 * 128)
    halves = [
        jnp.concatenate([mid[:, h * MIDH : (h + 1) * MIDH], out[h]], axis=1) for h in range(2)
    ]
    return jnp.stack(halves)


def per_device(latents, frames, offsets, assign, w_in, w_mid, w_out, gain_in, gain_mid, gain_out):
    groups = lax.axis_size("grp")
    row_index = lax.axis_index("row")
    group_index = lax.axis_index("grp")
    channels = w_in.shape[0]
    cap_vals = latents.shape[1] // groups
    cap_tokens = cap_vals // channels
    span_len = cap_tokens // FMAX

    weights = gather_weights(pack_weights(w_mid, w_out)).reshape(2, 8 * groups, HALF)
    win = w_in.transpose(1, 0, 2).reshape(27 * channels, C1)

    table = latents.reshape(128, 128)
    start = offsets[assign]
    length = frames[assign] * (span_len * channels)
    first = start // 8
    want = first[:, None] + jnp.arange(3, dtype=jnp.int32)[None, :]
    pick = (want.reshape(-1)[:, None] == jnp.arange(128, dtype=jnp.int32)[None, :]).astype(BF16)
    rows = jnp.dot(pick, table, preferred_element_type=F32).astype(BF16).reshape(groups, 384)
    shift = (start % 8)[:, None]
    for bit in (4, 2, 1):
        moved = jnp.pad(rows[:, 16 * bit :], ((0, 0), (0, 16 * bit)))
        rows = jnp.where((shift & bit) != 0, moved, rows)
    keep = jnp.arange(cap_vals, dtype=jnp.int32)[None, :] < length[:, None]
    outgoing = jnp.where(keep, rows[:, :cap_vals], jnp.zeros((), BF16))
    incoming = lax.all_to_all(outgoing, "grp", split_axis=0, concat_axis=0, tiled=True)

    tokens = incoming.reshape(groups * cap_tokens, channels)
    request = assign[group_index]
    count = frames[request]
    fill_len = count * span_len
    frame_ids = jnp.arange(FMAX, dtype=jnp.int32)[:, None, None]
    row_ids = row_index * RL - 2 + jnp.arange(6, dtype=jnp.int32)[None, :, None]
    col_ids = jnp.arange(WL, dtype=jnp.int32)[None, None, :]
    position = (frame_ids * 16 + row_ids) * WL + col_ids
    valid = (row_ids >= 0) & (row_ids < 16) & (frame_ids < count) & (col_ids >= 0)
    position = jnp.where(valid, position, 0)
    shard = jnp.minimum(position // fill_len, groups - 1)
    within = position % fill_len
    picked = tokens[(shard * cap_tokens + within).reshape(-1)]
    picked = jnp.where(valid.reshape(-1, 1), picked, jnp.zeros((), BF16))
    xt = jnp.pad(picked.T, ((0, 0), (320, 64)))
    info = jnp.stack([row_index.astype(jnp.int32), count])
    gout = jnp.pad(gain_out, (0, 128 - C3)).reshape(1, 128)
    return decode(
        info, xt, win, weights, gain_in.reshape(1, C1), gain_mid.reshape(1, C2), gout
    )


def solution(mesh):
    placed = (
        P("grp", None),
        P(),
        P(),
        P(),
        P(),
        P("grp", None, None),
        P("grp", None, None),
        P(),
        P(),
        P(),
    )
    return jax.shard_map(
        per_device,
        mesh=mesh,
        in_specs=placed,
        out_specs=P("grp", None, "row", None),
        check_vma=False,
    )
```

```python
import jax
import jax.numpy as jnp
from jax import lax
from jax.experimental import pallas as pl
from jax.experimental.pallas import tpu as pltpu
from jax.sharding import PartitionSpec as P

RL = 2
WL = 16
FMAX = 4
C1 = 384
C2 = 192
C3 = 96
C1P = 512
NB = 1792
MIDH = 3 * NB // 2
HALF = MIDH
OB = 896
MID_PARTS = (
    (0, 0, 0, 0, NB),
    (1, 0, NB, 0, NB // 2),
    (1, 1, 0, NB // 2, NB // 2),
    (2, 1, NB // 2, 0, NB),
)
EPS = 1e-06
F32 = jnp.float32
BF16 = jnp.bfloat16
MESH = pl.DeviceIdType.MESH


def silu_norm(h, gain, width):
    mean_sq = jnp.sum(h * h, axis=-1, keepdims=True) * (1.0 / width)
    v = h * lax.rsqrt(mean_sq + EPS) * gain
    return v / (1.0 + jnp.exp(-v))


def iota(shape, dim):
    return lax.broadcasted_iota(jnp.int32, shape, dim)


def decode_kernel(
    info, xt_ref, win_ref, w_ref, gin_ref, gmid_ref, gout_ref, o_ref,
    cols, act1, z1, act2, lhs, z2, flat,
):
    row = info[0]
    count = info[1]

    xt = xt_ref[...].astype(F32)
    lane = iota(xt.shape, 1) % WL
    shifted = (
        jnp.where(lane == WL - 1, 0.0, xt),
        xt,
        jnp.where(lane == 0, 0.0, xt),
    )
    width = xt.shape[1]
    for a in range(3):
        for b in range(3):
            for e in range(3):
                start = 320 + (a - 2) * 96 + (b - 1) * 16 + (e - 1)
                piece = pltpu.roll(shifted[e], width - start, 1)[:, :384]
                k = 9 * a + 3 * b + e
                cols[16 * k : 16 * k + 16, :] = piece.astype(BF16)
    h = lax.dot_general(
        cols[...], win_ref[...], (((0,), (0,)), ((), ())), preferred_element_type=F32
    )
    act = silu_norm(h, gin_ref[...], C1).astype(BF16)
    src = iota((C1, C1P), 0)
    dst = iota((C1, C1P), 1)
    place = ((dst // 8 * 6 + dst % 8 == src) & (dst % 8 < 6)).astype(F32).astype(BF16)
    spread = jnp.dot(act, place, preferred_element_type=F32)
    act1[0:128, :] = jnp.zeros((128, C1P), BF16)
    rid = 2 * row - 1 + iota((64, 1), 0) // WL
    keep = (rid >= 0) & (rid < 16)
    for t in range(FMAX):
        part = spread[t * 96 + 16 : t * 96 + 80, :]
        act1[128 + 64 * t : 192 + 64 * t, :] = jnp.where(keep, part, 0.0).astype(BF16)

    for a, half, start, at, size in MID_PARTS:
        part = jnp.dot(
            act1[64 * a : 64 * a + 256, :],
            w_ref[half, :, start : start + size],
            preferred_element_type=F32,
        )
        if a == 0:
            z1[:, at : at + size] = part
        else:
            z1[:, at : at + size] += part

    act2[0:384, :] = jnp.zeros((384, C2), BF16)
    xpos = iota((64, 1), 0) % WL
    gmid = gmid_ref[...]
    for t in range(FMAX):
        combos = []
        for b in range(3):
            z = []
            for e in range(3):
                k = 3 * b + e
                if k % 2 == 0:
                    z.append(z1[64 * t : 64 * t + 64, 192 * k : 192 * k + 192])
                else:
                    win = z1[64 * t : 64 * t + 64, 192 * k - 64 : 192 * k + 192]
                    z.append(pltpu.roll(win, 192, 1)[:, :192])
            left = jnp.where(xpos == 0, 0.0, pltpu.roll(z[0], 1, 0))
            right = jnp.where(xpos == WL - 1, 0.0, pltpu.roll(z[2], 63, 0))
            combos.append((left + z[1] + z[2], z[0] + z[1] + right))
        for m in range(6):
            y, p = (m + 1) // 2, (m + 1) % 2
            rows = (y, y, y + 1) if p else (y - 1, y, y)
            rid2 = 4 * row - 1 + m
            ok = (rid2 >= 0) & (rid2 < 32)
            for q in range(2):
                h = sum(combos[b][q][16 * rows[b] : 16 * rows[b] + 16, :] for b in range(3))
                v = jnp.where(ok, silu_norm(h, gmid, C2), 0.0)
                at = ((t + 2) * 12 + m * 2 + q) * 16
                act2[at : at + 16, :] = v.astype(BF16)

    src = iota((C2, 512), 0)
    dst = iota((C2, 512), 1)

    def place_out(pairs):
        hit = jnp.zeros((C2, 512), F32)
        for i, r in pairs:
            hit += ((dst % 8 == r) & (dst // 8 * 3 + i == src)).astype(F32)
        return hit.astype(BF16)

    first = place_out(((2, 6),))
    lhs[0] = jnp.dot(act2[...], place_out(((0, 6), (1, 7))), preferred_element_type=F32).astype(BF16)
    mixed = jnp.dot(act2[0:768, :], first, preferred_element_type=F32)
    mixed += jnp.dot(act2[192:960, :], place_out(((2, 7),)), preferred_element_type=F32)
    lhs[1, 0:768] = mixed.astype(BF16)
    z2[...] = jnp.dot(lhs[1, 0:768], w_ref[1, :, 0:OB], preferred_element_type=F32)
    last = jnp.dot(act2[384:1152, :], first, preferred_element_type=F32)
    lhs[1, 0:768] = last.astype(BF16)
    z2[...] += jnp.dot(lhs[1, 0:768], w_ref[1, :, OB : 2 * OB], preferred_element_type=F32)
    for a in range(3):
        z2[...] += jnp.dot(
            lhs[0, 192 * a : 192 * a + 768],
            w_ref[0, :, OB * a : OB * a + OB],
            preferred_element_type=F32,
        )

    xpos = iota((96, 1), 0) % WL
    gout = gout_ref[...]
    lanes = iota((64, 128), 1)
    for t in range(FMAX):
        combos = []
        for b in range(3):
            z = []
            for e in range(3):
                k = 3 * b + e
                at, off = C3 * k // 128 * 128, C3 * k % 128
                wide = 128 if off + C3 <= 128 else 256
                block = z2[192 * t : 192 * t + 192, at : at + wide]
                if off:
                    block = pltpu.roll(block, wide - off, 1)
                block = block[:, :128].reshape(6, 2, 16, 128)
                z.append((block[:, 0].reshape(96, 128), block[:, 1].reshape(96, 128)))
            left = (jnp.where(xpos == 0, 0.0, pltpu.roll(z[0][1], 1, 0)), z[0][0])
            right = (z[2][1], jnp.where(xpos == WL - 1, 0.0, pltpu.roll(z[2][0], 95, 0)))
            combos.append(
                [
                    (left[q] + z[1][q] + z[2][q], z[0][q] + z[1][q] + right[q])
                    for q in range(2)
                ]
            )
        for p in range(2):
            phases = []
            for q in range(2):
                for q2 in range(2):
                    c = [combos[b][q][q2] for b in range(3)]
                    if p:
                        h = c[0][16:80] + c[1][16:80] + c[2][32:96]
                    else:
                        h = c[0][0:64] + c[1][16:80] + c[2][16:80]
                    h = jnp.where(lanes < C3, h, 0.0)
                    phases.append(jnp.where(t < count, silu_norm(h, gout, C3), 0.0))
            r1 = pltpu.roll(phases[1], 96, 1)
            r2 = pltpu.roll(phases[2], 64, 1)
            r3 = pltpu.roll(phases[3], 32, 1)
            tiles = (
                jnp.where(lanes < 96, phases[0], r1),
                jnp.where(lanes < 64, r1, r2),
                jnp.where(lanes < 32, r2, r3),
            )
            for m in range(4):
                at = (t * 8 + 2 * m + p) * 16
                for j in range(3):
                    flat[j, at : at + 16, :] = tiles[j][16 * m : 16 * m + 16]
        for x in range(WL):
            for j in range(3):
                v = flat[j, pl.ds(t * 128 + x, 8, stride=16), :]
                at = x * 384 + j * 128
                o_ref[0, t, :, at : at + 128] = v.astype(BF16)


def decode(info, xt, win, weights, gin, gmid, gout):
    vm = pl.BlockSpec(memory_space=pltpu.VMEM)
    return pl.pallas_call(
        decode_kernel,
        name="decode",
        out_shape=jax.ShapeDtypeStruct((1, FMAX, 4 * RL, 4 * WL * C3), BF16),
        in_specs=[pl.BlockSpec(memory_space=pltpu.SMEM)] + [vm] * 6,
        out_specs=vm,
        scratch_shapes=[
            pltpu.VMEM((432, 384), BF16),
            pltpu.VMEM((384, C1P), BF16),
            pltpu.VMEM((256, NB), F32),
            pltpu.VMEM((1152, C2), BF16),
            pltpu.VMEM((2, 1152, 512), BF16),
            pltpu.VMEM((768, OB), F32),
            pltpu.VMEM((3, 512, 128), F32),
        ],
        compiler_params=pltpu.CompilerParams(vmem_limit_bytes=56 * 1024 * 1024),
    )(info, xt, win, weights, gin, gmid, gout)


def gather_kernel(
    x_ref, o_ref, g_ref, t_ref, m_ref, own_sem, send_sem, recv_sem, tok_local, tok_send, tok_recv
):
    grp = lax.axis_index("grp")
    row = lax.axis_index("row")
    core = row % 2
    step1 = 1 + 7 * core
    step2 = 8 - 7 * core
    i1 = (grp // step1) % 8
    i2 = (grp // step2) % 8

    def slot(a, b):
        return (a % 8) * step1 + (b % 8) * step2

    right1, left1 = (slot(i1 + 1, i2), row), (slot(i1 + 7, i2), row)
    right2, left2 = (slot(i1, i2 + 1), row), (slot(i1, i2 + 7), row)
    partner = (grp, row + 1 - 2 * core)

    y, z = grp % 8, grp // 8
    barrier = pltpu.get_barrier_semaphore()
    pl.semaphore_signal(barrier, inc=1, device_id=partner, device_id_type=MESH)
    for d in range(1, 8):
        for peer in (z * 8 + (y + d) % 8, (z + d) % 8 * 8 + y):
            pl.semaphore_signal(barrier, inc=1, device_id=(peer, row), device_id_type=MESH)
    pl.semaphore_wait(barrier, 15)

    started = []

    def send(way, peer, a, b, own=False):
        at = slot(a, b)
        copy = pltpu.make_async_remote_copy(
            src_ref=x_ref.at[core] if own else g_ref.at[core, at],
            dst_ref=g_ref.at[core, at],
            send_sem=send_sem.at[way, at],
            recv_sem=recv_sem.at[core, at],
            device_id=peer,
            device_id_type=MESH,
        )
        copy.start()
        started.append(copy)

    def arrived(half, at):
        pltpu.make_async_remote_copy(
            src_ref=g_ref.at[half, at],
            dst_ref=g_ref.at[half, at],
            send_sem=send_sem.at[0, at],
            recv_sem=recv_sem.at[half, at],
            device_id=partner,
            device_id_type=MESH,
        ).wait_recv()

    send(0, right1, i1, i2, True)
    send(1, left1, i1, i2, True)
    send(2, right2, i1, i2, True)
    send(3, left2, i1, i2, True)
    local = [
        pltpu.make_async_copy(x_ref.at[h], g_ref.at[h, grp], own_sem.at[h]) for h in range(2)
    ]
    for copy in local:
        copy.start()

    def tokens_y(d):
        return pltpu.make_async_remote_copy(
            src_ref=o_ref.at[:, (y + d) % 8],
            dst_ref=m_ref.at[y],
            send_sem=tok_send.at[0, d],
            recv_sem=tok_recv.at[0, d],
            device_id=(z * 8 + (y + d) % 8, row),
            device_id_type=MESH,
        )

    def tokens_z(d):
        return pltpu.make_async_remote_copy(
            src_ref=m_ref.at[:, (z + d) % 8],
            dst_ref=t_ref.at[z],
            send_sem=tok_send.at[1, d],
            recv_sem=tok_recv.at[1, d],
            device_id=((z + d) % 8 * 8 + y, row),
            device_id_type=MESH,
        )

    tok_own = pltpu.make_async_copy(o_ref.at[:, y], m_ref.at[y], tok_local.at[0])
    tok_own.start()
    for d in range(1, 8):
        tokens_y(d).start()

    line = [0, -1, 1, -2, 2, -3, 3, -4]
    for off in line[1:]:
        arrived(core, slot(i1 + off + 8, i2))
        if -4 < off < 0:
            send(0, right1, i1 + off + 8, i2)
        if 0 < off < 3:
            send(1, left1, i1 + off + 8, i2)
        send(2, right2, i1 + off + 8, i2)
        send(3, left2, i1 + off + 8, i2)
        send(4, partner, i1 + off + 8, i2)

    tok_own.wait()
    for d in range(1, 8):
        tokens_y(d).wait()
    tok_own = pltpu.make_async_copy(m_ref.at[:, z], t_ref.at[z], tok_local.at[1])
    tok_own.start()
    for d in range(1, 8):
        tokens_z(d).start()

    for dist in range(1, 5):
        for n, off in enumerate(line):
            a = i1 + off + 8
            for sign in (-1, 1):
                if dist == 4 and (n % 2 == 0) != (sign < 0):
                    continue
                b = i2 + sign * dist + 8
                arrived(core, slot(a, b))
                if dist < 3 or (dist == 3 and (n % 2 == 0) == (sign < 0)):
                    send(2 if sign < 0 else 3, right2 if sign < 0 else left2, a, b)
                send(4, partner, a, b)

    for n in range(1, 64):
        arrived(1 - core, (grp + n) % 64)
    for copy in started:
        copy.wait_send()
    for copy in local:
        copy.wait()
    tok_own.wait()
    for d in range(1, 8):
        tokens_z(d).wait()


def exchange(x, outgoing):
    any_spec = pl.BlockSpec(memory_space=pl.ANY)
    block = jax.ShapeDtypeStruct((8, 8, 2, 128), BF16)
    return pl.pallas_call(
        gather_kernel,
        name="exchange",
        out_shape=(jax.ShapeDtypeStruct((2, 64, 8, HALF), BF16), block, block),
        in_specs=[any_spec] * 2,
        out_specs=(any_spec,) * 3,
        scratch_shapes=[
            pltpu.SemaphoreType.DMA((2,)),
            pltpu.SemaphoreType.DMA((5, 64)),
            pltpu.SemaphoreType.DMA((2, 64)),
            pltpu.SemaphoreType.DMA((2,)),
            pltpu.SemaphoreType.DMA((2, 8)),
            pltpu.SemaphoreType.DMA((2, 8)),
        ],
        compiler_params=pltpu.CompilerParams(collective_id=0, has_side_effects=True),
    )(x, outgoing)


def pack_weights(w_mid, w_out):
    mid = jnp.pad(w_mid.reshape(6, 3, 9 * C2), ((0, 0), (0, 0), (0, NB - 9 * C2)))
    out = jnp.pad(w_out.reshape(3, 3, 9 * C3), ((0, 0), (0, 0), (0, OB - 9 * C3)))
    none = jnp.zeros((OB,), BF16)
    extra = [out[0, 0], out[0, 1], out[0, 2], out[2, 0], out[2, 2], none]
    extra += [out[1, 0], out[1, 1], out[1, 2], out[2, 1], none, none]
    extra = jnp.concatenate(extra).reshape(2, 3 * NB)
    piece = jnp.concatenate([mid.reshape(6, 3 * NB), extra], axis=0)
    return jnp.stack([piece[:, :HALF], piece[:, HALF:]])


def per_device(latents, frames, offsets, assign, w_in, w_mid, w_out, gain_in, gain_mid, gain_out):
    groups = lax.axis_size("grp")
    row_index = lax.axis_index("row")
    group_index = lax.axis_index("grp")
    channels = w_in.shape[0]
    cap_vals = latents.shape[1] // groups
    cap_tokens = cap_vals // channels
    span_len = cap_tokens // FMAX

    win = w_in.transpose(1, 0, 2).reshape(27 * channels, C1)

    table = latents.reshape(128, 128)
    start = offsets[assign]
    length = frames[assign] * (span_len * channels)
    first = start // 8
    want = first[:, None] + jnp.arange(3, dtype=jnp.int32)[None, :]
    pick = (want.reshape(-1)[:, None] == jnp.arange(128, dtype=jnp.int32)[None, :]).astype(BF16)
    rows = jnp.dot(pick, table, preferred_element_type=F32).astype(BF16).reshape(groups, 384)
    shift = (start % 8)[:, None]
    for bit in (4, 2, 1):
        moved = jnp.pad(rows[:, 16 * bit :], ((0, 0), (0, 16 * bit)))
        rows = jnp.where((shift & bit) != 0, moved, rows)
    keep = jnp.arange(cap_vals, dtype=jnp.int32)[None, :] < length[:, None]
    outgoing = jnp.where(keep, rows[:, :cap_vals], jnp.zeros((), BF16))
    weights, incoming, _ = exchange(pack_weights(w_mid, w_out), outgoing.reshape(8, 8, 2, 128))
    weights = weights.reshape(2, 8 * groups, HALF)

    tokens = incoming.reshape(groups * cap_tokens, channels)
    mine = jnp.arange(groups, dtype=jnp.int32) == group_index
    count = jnp.sum(jnp.where(mine, frames[assign], 0))
    fill_len = count * span_len
    frame_ids = jnp.arange(FMAX, dtype=jnp.int32)[:, None, None]
    row_ids = row_index * RL - 2 + jnp.arange(6, dtype=jnp.int32)[None, :, None]
    col_ids = jnp.arange(WL, dtype=jnp.int32)[None, None, :]
    position = (frame_ids * 16 + row_ids) * WL + col_ids
    valid = (row_ids >= 0) & (row_ids < 16) & (frame_ids < count) & (col_ids >= 0)
    position = jnp.where(valid, position, 0)
    shard = jnp.minimum(position // fill_len, groups - 1)
    within = position % fill_len
    picked = tokens[(shard * cap_tokens + within).reshape(-1)]
    picked = jnp.where(valid.reshape(-1, 1), picked, jnp.zeros((), BF16))
    xt = jnp.pad(picked.T, ((0, 0), (320, 64)))
    info = jnp.stack([row_index.astype(jnp.int32), count])
    gout = jnp.pad(gain_out, (0, 128 - C3)).reshape(1, 128)
    return decode(
        info, xt, win, weights, gain_in.reshape(1, C1), gain_mid.reshape(1, C2), gout
    )


def solution(mesh):
    placed = (
        P("grp", None),
        P(),
        P(),
        P(),
        P(),
        P("grp", None, None),
        P("grp", None, None),
        P(),
        P(),
        P(),
    )
    return jax.shard_map(
        per_device,
        mesh=mesh,
        in_specs=placed,
        out_specs=P("grp", None, "row", None),
        check_vma=False,
    )
```

```python
import jax
import jax.numpy as jnp
from jax import lax
from jax.experimental import pallas as pl
from jax.experimental.pallas import tpu as pltpu
from jax.sharding import PartitionSpec as P

RL = 2
WL = 16
FMAX = 4
C1 = 384
C2 = 192
C3 = 96
C1P = 512
NB = 1792
MIDH = 3 * NB // 2
HALF = MIDH
OB = 896
MID_PARTS = (
    (0, 0, 0, 0, NB),
    (1, 0, NB, 0, NB // 2),
    (1, 1, 0, NB // 2, NB // 2),
    (2, 1, NB // 2, 0, NB),
)
EPS = 1e-06
F32 = jnp.float32
BF16 = jnp.bfloat16
MESH = pl.DeviceIdType.MESH


def silu_norm(h, gain, width):
    mean_sq = jnp.sum(h * h, axis=-1, keepdims=True) * (1.0 / width)
    v = h * lax.rsqrt(mean_sq + EPS) * gain
    return v / (1.0 + jnp.exp(-v))


def iota(shape, dim):
    return lax.broadcasted_iota(jnp.int32, shape, dim)


def decode_kernel(
    info, xt_ref, win_ref, w_ref, gin_ref, gmid_ref, gout_ref, o_ref,
    cols, act1, z1, act2, lhs, z2, flat,
):
    row = info[0]
    count = info[1]

    xt = xt_ref[...].astype(F32)
    lane = iota(xt.shape, 1) % WL
    shifted = (
        jnp.where(lane == WL - 1, 0.0, xt),
        xt,
        jnp.where(lane == 0, 0.0, xt),
    )
    width = xt.shape[1]
    for a in range(3):
        for b in range(3):
            for e in range(3):
                start = 320 + (a - 2) * 96 + (b - 1) * 16 + (e - 1)
                piece = pltpu.roll(shifted[e], width - start, 1)[:, :384]
                k = 9 * a + 3 * b + e
                cols[16 * k : 16 * k + 16, :] = piece.astype(BF16)
    h = lax.dot_general(
        cols[...], win_ref[...], (((0,), (0,)), ((), ())), preferred_element_type=F32
    )
    act = silu_norm(h, gin_ref[...], C1).astype(BF16)
    src = iota((C1, C1P), 0)
    dst = iota((C1, C1P), 1)
    place = ((dst // 8 * 6 + dst % 8 == src) & (dst % 8 < 6)).astype(F32).astype(BF16)
    spread = jnp.dot(act, place, preferred_element_type=F32)
    act1[0:128, :] = jnp.zeros((128, C1P), BF16)
    rid = 2 * row - 1 + iota((64, 1), 0) // WL
    keep = (rid >= 0) & (rid < 16)
    for t in range(FMAX):
        part = spread[t * 96 + 16 : t * 96 + 80, :]
        act1[128 + 64 * t : 192 + 64 * t, :] = jnp.where(keep, part, 0.0).astype(BF16)

    for a, half, start, at, size in MID_PARTS:
        part = jnp.dot(
            act1[64 * a : 64 * a + 256, :],
            w_ref[half, :, start : start + size],
            preferred_element_type=F32,
        )
        if a == 0:
            z1[:, at : at + size] = part
        else:
            z1[:, at : at + size] += part

    act2[0:384, :] = jnp.zeros((384, C2), BF16)
    xpos = iota((64, 1), 0) % WL
    gmid = gmid_ref[...]
    for t in range(FMAX):
        combos = []
        for b in range(3):
            z = []
            for e in range(3):
                k = 3 * b + e
                if k % 2 == 0:
                    z.append(z1[64 * t : 64 * t + 64, 192 * k : 192 * k + 192])
                else:
                    win = z1[64 * t : 64 * t + 64, 192 * k - 64 : 192 * k + 192]
                    z.append(pltpu.roll(win, 192, 1)[:, :192])
            left = jnp.where(xpos == 0, 0.0, pltpu.roll(z[0], 1, 0))
            right = jnp.where(xpos == WL - 1, 0.0, pltpu.roll(z[2], 63, 0))
            combos.append((left + z[1] + z[2], z[0] + z[1] + right))
        for m in range(6):
            y, p = (m + 1) // 2, (m + 1) % 2
            rows = (y, y, y + 1) if p else (y - 1, y, y)
            rid2 = 4 * row - 1 + m
            ok = (rid2 >= 0) & (rid2 < 32)
            for q in range(2):
                h = sum(combos[b][q][16 * rows[b] : 16 * rows[b] + 16, :] for b in range(3))
                v = jnp.where(ok, silu_norm(h, gmid, C2), 0.0)
                at = ((t + 2) * 12 + m * 2 + q) * 16
                act2[at : at + 16, :] = v.astype(BF16)

    src = iota((C2, 512), 0)
    dst = iota((C2, 512), 1)

    def place_out(pairs):
        hit = jnp.zeros((C2, 512), F32)
        for i, r in pairs:
            hit += ((dst % 8 == r) & (dst // 8 * 3 + i == src)).astype(F32)
        return hit.astype(BF16)

    first = place_out(((2, 6),))
    lhs[0] = jnp.dot(act2[...], place_out(((0, 6), (1, 7))), preferred_element_type=F32).astype(BF16)
    mixed = jnp.dot(act2[0:768, :], first, preferred_element_type=F32)
    mixed += jnp.dot(act2[192:960, :], place_out(((2, 7),)), preferred_element_type=F32)
    lhs[1, 0:768] = mixed.astype(BF16)
    z2[...] = jnp.dot(lhs[1, 0:768], w_ref[1, :, 0:OB], preferred_element_type=F32)
    last = jnp.dot(act2[384:1152, :], first, preferred_element_type=F32)
    lhs[1, 0:768] = last.astype(BF16)
    z2[...] += jnp.dot(lhs[1, 0:768], w_ref[1, :, OB : 2 * OB], preferred_element_type=F32)
    for a in range(3):
        z2[...] += jnp.dot(
            lhs[0, 192 * a : 192 * a + 768],
            w_ref[0, :, OB * a : OB * a + OB],
            preferred_element_type=F32,
        )

    xpos = iota((96, 1), 0) % WL
    gout = gout_ref[...]
    lanes = iota((64, 128), 1)
    for t in range(FMAX):
        combos = []
        for b in range(3):
            z = []
            for e in range(3):
                k = 3 * b + e
                at, off = C3 * k // 128 * 128, C3 * k % 128
                wide = 128 if off + C3 <= 128 else 256
                block = z2[192 * t : 192 * t + 192, at : at + wide]
                if off:
                    block = pltpu.roll(block, wide - off, 1)
                block = block[:, :128].reshape(6, 2, 16, 128)
                z.append((block[:, 0].reshape(96, 128), block[:, 1].reshape(96, 128)))
            left = (jnp.where(xpos == 0, 0.0, pltpu.roll(z[0][1], 1, 0)), z[0][0])
            right = (z[2][1], jnp.where(xpos == WL - 1, 0.0, pltpu.roll(z[2][0], 95, 0)))
            combos.append(
                [
                    (left[q] + z[1][q] + z[2][q], z[0][q] + z[1][q] + right[q])
                    for q in range(2)
                ]
            )
        for p in range(2):
            phases = []
            for q in range(2):
                for q2 in range(2):
                    c = [combos[b][q][q2] for b in range(3)]
                    if p:
                        h = c[0][16:80] + c[1][16:80] + c[2][32:96]
                    else:
                        h = c[0][0:64] + c[1][16:80] + c[2][16:80]
                    h = jnp.where(lanes < C3, h, 0.0)
                    phases.append(jnp.where(t < count, silu_norm(h, gout, C3), 0.0))
            r1 = pltpu.roll(phases[1], 96, 1)
            r2 = pltpu.roll(phases[2], 64, 1)
            r3 = pltpu.roll(phases[3], 32, 1)
            tiles = (
                jnp.where(lanes < 96, phases[0], r1),
                jnp.where(lanes < 64, r1, r2),
                jnp.where(lanes < 32, r2, r3),
            )
            for m in range(4):
                at = (t * 8 + 2 * m + p) * 16
                for j in range(3):
                    flat[j, at : at + 16, :] = tiles[j][16 * m : 16 * m + 16]
        for x in range(WL):
            for j in range(3):
                v = flat[j, pl.ds(t * 128 + x, 8, stride=16), :]
                at = x * 384 + j * 128
                o_ref[0, t, :, at : at + 128] = v.astype(BF16)


def decode(info, xt, win, weights, gin, gmid, gout):
    vm = pl.BlockSpec(memory_space=pltpu.VMEM)
    return pl.pallas_call(
        decode_kernel,
        name="decode",
        out_shape=jax.ShapeDtypeStruct((1, FMAX, 4 * RL, 4 * WL * C3), BF16),
        in_specs=[pl.BlockSpec(memory_space=pltpu.SMEM)] + [vm] * 6,
        out_specs=vm,
        scratch_shapes=[
            pltpu.VMEM((432, 384), BF16),
            pltpu.VMEM((384, C1P), BF16),
            pltpu.VMEM((256, NB), F32),
            pltpu.VMEM((1152, C2), BF16),
            pltpu.VMEM((2, 1152, 512), BF16),
            pltpu.VMEM((768, OB), F32),
            pltpu.VMEM((3, 512, 128), F32),
        ],
        compiler_params=pltpu.CompilerParams(vmem_limit_bytes=56 * 1024 * 1024),
    )(info, xt, win, weights, gin, gmid, gout)


def gather_kernel(
    x_ref, o_ref, g_ref, t_ref, m_ref, own_sem, send_sem, recv_sem, tok_local, tok_send, tok_recv
):
    grp = lax.axis_index("grp")
    row = lax.axis_index("row")
    core = row % 2
    step1 = 1 + 7 * core
    step2 = 8 - 7 * core
    i1 = (grp // step1) % 8
    i2 = (grp // step2) % 8

    def slot(a, b):
        return (a % 8) * step1 + (b % 8) * step2

    right2, left2 = (slot(i1, i2 + 1), row), (slot(i1, i2 + 7), row)
    partner = (grp, row + 1 - 2 * core)

    y, z = grp % 8, grp // 8
    barrier = pltpu.get_barrier_semaphore()
    pl.semaphore_signal(barrier, inc=1, device_id=partner, device_id_type=MESH)
    for d in range(1, 8):
        for peer in (z * 8 + (y + d) % 8, (z + d) % 8 * 8 + y):
            pl.semaphore_signal(barrier, inc=1, device_id=(peer, row), device_id_type=MESH)
    pl.semaphore_wait(barrier, 15)

    started = []

    def send(way, peer, a, b, own=False, tag=None):
        at = slot(a, b)
        copy = pltpu.make_async_remote_copy(
            src_ref=x_ref.at[core] if own else g_ref.at[core, at],
            dst_ref=g_ref.at[core, at],
            send_sem=send_sem.at[way, at if tag is None else tag],
            recv_sem=recv_sem.at[core, at],
            device_id=peer,
            device_id_type=MESH,
        )
        copy.start()
        started.append(copy)

    def arrived(half, at):
        pltpu.make_async_remote_copy(
            src_ref=g_ref.at[half, at],
            dst_ref=g_ref.at[half, at],
            send_sem=send_sem.at[0, at],
            recv_sem=recv_sem.at[half, at],
            device_id=partner,
            device_id_type=MESH,
        ).wait_recv()

    for d in (1, 7, 2, 6, 3, 5, 4):
        send(0, (slot(i1 + d, i2), row), i1, i2, True, tag=d)
    send(1, right2, i1, i2, True)
    send(2, left2, i1, i2, True)
    local = [
        pltpu.make_async_copy(x_ref.at[h], g_ref.at[h, grp], own_sem.at[h]) for h in range(2)
    ]
    for copy in local:
        copy.start()

    def tokens_y(d):
        return pltpu.make_async_remote_copy(
            src_ref=o_ref.at[:, (y + d) % 8],
            dst_ref=m_ref.at[y],
            send_sem=tok_send.at[0, d],
            recv_sem=tok_recv.at[0, d],
            device_id=(z * 8 + (y + d) % 8, row),
            device_id_type=MESH,
        )

    def tokens_z(d):
        return pltpu.make_async_remote_copy(
            src_ref=m_ref.at[:, (z + d) % 8],
            dst_ref=t_ref.at[z],
            send_sem=tok_send.at[1, d],
            recv_sem=tok_recv.at[1, d],
            device_id=((z + d) % 8 * 8 + y, row),
            device_id_type=MESH,
        )

    tok_own = pltpu.make_async_copy(o_ref.at[:, y], m_ref.at[y], tok_local.at[0])
    tok_own.start()
    for d in range(1, 8):
        tokens_y(d).start()

    line = [0, -1, 1, -2, 2, -3, 3, -4]
    for off in line[1:]:
        arrived(core, slot(i1 + off + 8, i2))
        send(1, right2, i1 + off + 8, i2)
        send(2, left2, i1 + off + 8, i2)
        send(3, partner, i1 + off + 8, i2)

    tok_own.wait()
    for d in range(1, 8):
        tokens_y(d).wait()
    tok_own = pltpu.make_async_copy(m_ref.at[:, z], t_ref.at[z], tok_local.at[1])
    tok_own.start()
    for d in range(1, 8):
        tokens_z(d).start()

    for dist in range(1, 5):
        for n, off in enumerate(line):
            a = i1 + off + 8
            for sign in (-1, 1):
                if dist == 4 and (n % 2 == 0) != (sign < 0):
                    continue
                b = i2 + sign * dist + 8
                arrived(core, slot(a, b))
                if dist < 3 or (dist == 3 and (n % 2 == 0) == (sign < 0)):
                    send(1 if sign < 0 else 2, right2 if sign < 0 else left2, a, b)
                send(3, partner, a, b)

    for n in range(1, 64):
        arrived(1 - core, (grp + n) % 64)
    for copy in started:
        copy.wait_send()
    for copy in local:
        copy.wait()
    tok_own.wait()
    for d in range(1, 8):
        tokens_z(d).wait()


def exchange(x, outgoing):
    any_spec = pl.BlockSpec(memory_space=pl.ANY)
    vm_spec = pl.BlockSpec(memory_space=pltpu.VMEM)
    block = jax.ShapeDtypeStruct((8, 8, 2, 128), BF16)
    return pl.pallas_call(
        gather_kernel,
        name="exchange",
        out_shape=(jax.ShapeDtypeStruct((2, 64, 8, HALF), BF16), block, block),
        in_specs=[vm_spec, any_spec],
        out_specs=(vm_spec, any_spec, any_spec),
        scratch_shapes=[
            pltpu.SemaphoreType.DMA((2,)),
            pltpu.SemaphoreType.DMA((4, 64)),
            pltpu.SemaphoreType.DMA((2, 64)),
            pltpu.SemaphoreType.DMA((2,)),
            pltpu.SemaphoreType.DMA((2, 8)),
            pltpu.SemaphoreType.DMA((2, 8)),
        ],
        compiler_params=pltpu.CompilerParams(collective_id=0, has_side_effects=True),
    )(x, outgoing)


def pack_weights(w_mid, w_out):
    mid = jnp.pad(w_mid.reshape(6, 3, 9 * C2), ((0, 0), (0, 0), (0, NB - 9 * C2)))
    out = jnp.pad(w_out.reshape(3, 3, 9 * C3), ((0, 0), (0, 0), (0, OB - 9 * C3)))
    none = jnp.zeros((OB,), BF16)
    extra = [out[0, 0], out[0, 1], out[0, 2], out[2, 0], out[2, 2], none]
    extra += [out[1, 0], out[1, 1], out[1, 2], out[2, 1], none, none]
    extra = jnp.concatenate(extra).reshape(2, 3 * NB)
    piece = jnp.concatenate([mid.reshape(6, 3 * NB), extra], axis=0)
    return jnp.stack([piece[:, :HALF], piece[:, HALF:]])


def per_device(latents, frames, offsets, assign, w_in, w_mid, w_out, gain_in, gain_mid, gain_out):
    groups = lax.axis_size("grp")
    row_index = lax.axis_index("row")
    group_index = lax.axis_index("grp")
    channels = w_in.shape[0]
    cap_vals = latents.shape[1] // groups
    cap_tokens = cap_vals // channels
    span_len = cap_tokens // FMAX

    win = w_in.transpose(1, 0, 2).reshape(27 * channels, C1)

    table = latents.reshape(128, 128)
    packed = (offsets * 8 + frames).at[assign].get(mode="promise_in_bounds")
    start = packed // 8
    lasting = packed % 8
    length = lasting * (span_len * channels)
    first = start // 8
    want = first[:, None] + jnp.arange(3, dtype=jnp.int32)[None, :]
    pick = (want.reshape(-1)[:, None] == jnp.arange(128, dtype=jnp.int32)[None, :]).astype(BF16)
    rows = jnp.dot(pick, table, preferred_element_type=F32).astype(BF16).reshape(groups, 384)
    shift = (start % 8)[:, None]
    for bit in (4, 2, 1):
        moved = jnp.pad(rows[:, 16 * bit :], ((0, 0), (0, 16 * bit)))
        rows = jnp.where((shift & bit) != 0, moved, rows)
    keep = jnp.arange(cap_vals, dtype=jnp.int32)[None, :] < length[:, None]
    outgoing = jnp.where(keep, rows[:, :cap_vals], jnp.zeros((), BF16))
    weights, incoming, _ = exchange(pack_weights(w_mid, w_out), outgoing.reshape(8, 8, 2, 128))
    weights = weights.reshape(2, 8 * groups, HALF)

    tokens = incoming.reshape(groups * cap_tokens, channels)
    mine = jnp.arange(groups, dtype=jnp.int32) == group_index
    count = jnp.sum(jnp.where(mine, lasting, 0))
    fill_len = count * span_len
    frame_ids = jnp.arange(FMAX, dtype=jnp.int32)[:, None, None]
    row_ids = row_index * RL - 2 + jnp.arange(6, dtype=jnp.int32)[None, :, None]
    col_ids = jnp.arange(WL, dtype=jnp.int32)[None, None, :]
    position = (frame_ids * 16 + row_ids) * WL + col_ids
    valid = (row_ids >= 0) & (row_ids < 16) & (frame_ids < count) & (col_ids >= 0)
    position = jnp.where(valid, position, 0)
    shard = jnp.minimum(position // fill_len, groups - 1)
    within = position % fill_len
    picked = tokens[(shard * cap_tokens + within).reshape(-1)]
    picked = jnp.where(valid.reshape(-1, 1), picked, jnp.zeros((), BF16))
    xt = jnp.pad(picked.T, ((0, 0), (320, 64)))
    info = jnp.stack([row_index.astype(jnp.int32), count])
    gout = jnp.pad(gain_out, (0, 128 - C3)).reshape(1, 128)
    return decode(
        info, xt, win, weights, gain_in.reshape(1, C1), gain_mid.reshape(1, C2), gout
    )


def solution(mesh):
    placed = (
        P("grp", None),
        P(),
        P(),
        P(),
        P(),
        P("grp", None, None),
        P("grp", None, None),
        P(),
        P(),
        P(),
    )
    return jax.shard_map(
        per_device,
        mesh=mesh,
        in_specs=placed,
        out_specs=P("grp", None, "row", None),
        check_vma=False,
    )
```

```python
import jax
import jax.numpy as jnp
from jax import lax
from jax.experimental import pallas as pl
from jax.experimental.pallas import tpu as pltpu
from jax.sharding import PartitionSpec as P

RL = 2
WL = 16
FMAX = 4
C1 = 384
C2 = 192
C3 = 96
C1P = 512
NB = 1792
MIDH = 3 * NB // 2
HALF = MIDH
OB = 896
MID_PARTS = (
    (0, 0, 0, 0, NB),
    (1, 0, NB, 0, NB // 2),
    (1, 1, 0, NB // 2, NB // 2),
    (2, 1, NB // 2, 0, NB),
)
EPS = 1e-06
F32 = jnp.float32
BF16 = jnp.bfloat16
MESH = pl.DeviceIdType.MESH


def silu_norm(h, gain, width):
    mean_sq = jnp.sum(h * h, axis=-1, keepdims=True) * (1.0 / width)
    v = h * lax.rsqrt(mean_sq + EPS) * gain
    return v / (1.0 + jnp.exp(-v))


def iota(shape, dim):
    return lax.broadcasted_iota(jnp.int32, shape, dim)


def decode_kernel(
    info, xt_ref, win_ref, w_ref, gin_ref, gmid_ref, gout_ref, o_ref,
    cols, act1, z1, act2, lhs, z2, flat,
):
    row = info[0]
    count = info[1]

    xt = xt_ref[...].astype(F32)
    lane = iota(xt.shape, 1) % WL
    shifted = (
        jnp.where(lane == WL - 1, 0.0, xt),
        xt,
        jnp.where(lane == 0, 0.0, xt),
    )
    width = xt.shape[1]
    for a in range(3):
        for b in range(3):
            for e in range(3):
                start = 320 + (a - 2) * 96 + (b - 1) * 16 + (e - 1)
                piece = pltpu.roll(shifted[e], width - start, 1)[:, :384]
                k = 9 * a + 3 * b + e
                cols[16 * k : 16 * k + 16, :] = piece.astype(BF16)
    h = lax.dot_general(
        cols[...], win_ref[...], (((0,), (0,)), ((), ())), preferred_element_type=F32
    )
    act = silu_norm(h, gin_ref[...].reshape(1, -1), C1).astype(BF16)
    src = iota((C1, C1P), 0)
    dst = iota((C1, C1P), 1)
    place = ((dst // 8 * 6 + dst % 8 == src) & (dst % 8 < 6)).astype(F32).astype(BF16)
    spread = jnp.dot(act, place, preferred_element_type=F32)
    act1[0:128, :] = jnp.zeros((128, C1P), BF16)
    rid = 2 * row - 1 + iota((64, 1), 0) // WL
    keep = (rid >= 0) & (rid < 16)
    for t in range(FMAX):
        part = spread[t * 96 + 16 : t * 96 + 80, :]
        act1[128 + 64 * t : 192 + 64 * t, :] = jnp.where(keep, part, 0.0).astype(BF16)

    for a, half, start, at, size in MID_PARTS:
        part = jnp.dot(
            act1[64 * a : 64 * a + 256, :],
            w_ref[half, :, start : start + size],
            preferred_element_type=F32,
        )
        if a == 0:
            z1[:, at : at + size] = part
        else:
            z1[:, at : at + size] += part

    act2[0:384, :] = jnp.zeros((384, C2), BF16)
    xpos = iota((64, 1), 0) % WL
    gmid = gmid_ref[...].reshape(1, -1)
    for t in range(FMAX):
        combos = []
        for b in range(3):
            z = []
            for e in range(3):
                k = 3 * b + e
                if k % 2 == 0:
                    z.append(z1[64 * t : 64 * t + 64, 192 * k : 192 * k + 192])
                else:
                    win = z1[64 * t : 64 * t + 64, 192 * k - 64 : 192 * k + 192]
                    z.append(pltpu.roll(win, 192, 1)[:, :192])
            left = jnp.where(xpos == 0, 0.0, pltpu.roll(z[0], 1, 0))
            right = jnp.where(xpos == WL - 1, 0.0, pltpu.roll(z[2], 63, 0))
            combos.append((left + z[1] + z[2], z[0] + z[1] + right))
        for m in range(6):
            y, p = (m + 1) // 2, (m + 1) % 2
            rows = (y, y, y + 1) if p else (y - 1, y, y)
            rid2 = 4 * row - 1 + m
            ok = (rid2 >= 0) & (rid2 < 32)
            for q in range(2):
                h = sum(combos[b][q][16 * rows[b] : 16 * rows[b] + 16, :] for b in range(3))
                v = jnp.where(ok, silu_norm(h, gmid, C2), 0.0)
                at = ((t + 2) * 12 + m * 2 + q) * 16
                act2[at : at + 16, :] = v.astype(BF16)

    src = iota((C2, 512), 0)
    dst = iota((C2, 512), 1)

    def place_out(pairs):
        hit = jnp.zeros((C2, 512), F32)
        for i, r in pairs:
            hit += ((dst % 8 == r) & (dst // 8 * 3 + i == src)).astype(F32)
        return hit.astype(BF16)

    first = place_out(((2, 6),))
    lhs[0] = jnp.dot(act2[...], place_out(((0, 6), (1, 7))), preferred_element_type=F32).astype(BF16)
    mixed = jnp.dot(act2[0:768, :], first, preferred_element_type=F32)
    mixed += jnp.dot(act2[192:960, :], place_out(((2, 7),)), preferred_element_type=F32)
    lhs[1, 0:768] = mixed.astype(BF16)
    z2[...] = jnp.dot(lhs[1, 0:768], w_ref[1, :, 0:OB], preferred_element_type=F32)
    last = jnp.dot(act2[384:1152, :], first, preferred_element_type=F32)
    lhs[1, 0:768] = last.astype(BF16)
    z2[...] += jnp.dot(lhs[1, 0:768], w_ref[1, :, OB : 2 * OB], preferred_element_type=F32)
    for a in range(3):
        z2[...] += jnp.dot(
            lhs[0, 192 * a : 192 * a + 768],
            w_ref[0, :, OB * a : OB * a + OB],
            preferred_element_type=F32,
        )

    xpos = iota((96, 1), 0) % WL
    gout = gout_ref[...]
    lanes = iota((64, 128), 1)
    for t in range(FMAX):
        combos = []
        for b in range(3):
            z = []
            for e in range(3):
                k = 3 * b + e
                at, off = C3 * k // 128 * 128, C3 * k % 128
                wide = 128 if off + C3 <= 128 else 256
                block = z2[192 * t : 192 * t + 192, at : at + wide]
                if off:
                    block = pltpu.roll(block, wide - off, 1)
                block = block[:, :128].reshape(6, 2, 16, 128)
                z.append((block[:, 0].reshape(96, 128), block[:, 1].reshape(96, 128)))
            left = (jnp.where(xpos == 0, 0.0, pltpu.roll(z[0][1], 1, 0)), z[0][0])
            right = (z[2][1], jnp.where(xpos == WL - 1, 0.0, pltpu.roll(z[2][0], 95, 0)))
            combos.append(
                [
                    (left[q] + z[1][q] + z[2][q], z[0][q] + z[1][q] + right[q])
                    for q in range(2)
                ]
            )
        for p in range(2):
            phases = []
            for q in range(2):
                for q2 in range(2):
                    c = [combos[b][q][q2] for b in range(3)]
                    if p:
                        h = c[0][16:80] + c[1][16:80] + c[2][32:96]
                    else:
                        h = c[0][0:64] + c[1][16:80] + c[2][16:80]
                    h = jnp.where(lanes < C3, h, 0.0)
                    phases.append(jnp.where(t < count, silu_norm(h, gout, C3), 0.0))
            r1 = pltpu.roll(phases[1], 96, 1)
            r2 = pltpu.roll(phases[2], 64, 1)
            r3 = pltpu.roll(phases[3], 32, 1)
            tiles = (
                jnp.where(lanes < 96, phases[0], r1),
                jnp.where(lanes < 64, r1, r2),
                jnp.where(lanes < 32, r2, r3),
            )
            for m in range(4):
                at = (t * 8 + 2 * m + p) * 16
                for j in range(3):
                    flat[j, at : at + 16, :] = tiles[j][16 * m : 16 * m + 16]
        for x in range(WL):
            for j in range(3):
                v = flat[j, pl.ds(t * 128 + x, 8, stride=16), :]
                at = x * 384 + j * 128
                o_ref[0, t, :, at : at + 128] = v.astype(BF16)


def decode(info, xt, win, weights, gin, gmid, gout):
    vm = pl.BlockSpec(memory_space=pltpu.VMEM)
    return pl.pallas_call(
        decode_kernel,
        name="decode",
        out_shape=jax.ShapeDtypeStruct((1, FMAX, 4 * RL, 4 * WL * C3), BF16),
        in_specs=[pl.BlockSpec(memory_space=pltpu.SMEM)] + [vm] * 6,
        out_specs=vm,
        scratch_shapes=[
            pltpu.VMEM((432, 384), BF16),
            pltpu.VMEM((384, C1P), BF16),
            pltpu.VMEM((256, NB), F32),
            pltpu.VMEM((1152, C2), BF16),
            pltpu.VMEM((2, 1152, 512), BF16),
            pltpu.VMEM((768, OB), F32),
            pltpu.VMEM((3, 512, 128), F32),
        ],
        compiler_params=pltpu.CompilerParams(vmem_limit_bytes=56 * 1024 * 1024),
    )(info, xt, win, weights, gin, gmid, gout)


def gather_kernel(
    x_ref, o_ref, g_ref, t_ref, m_ref, own_sem, send_sem, recv_sem, tok_local, tok_send, tok_recv
):
    grp = lax.axis_index("grp")
    row = lax.axis_index("row")
    core = row % 2
    step1 = 1 + 7 * core
    step2 = 8 - 7 * core
    i1 = (grp // step1) % 8
    i2 = (grp // step2) % 8

    def slot(a, b):
        return (a % 8) * step1 + (b % 8) * step2

    right2, left2 = (slot(i1, i2 + 1), row), (slot(i1, i2 + 7), row)
    partner = (grp, row + 1 - 2 * core)

    y, z = grp % 8, grp // 8
    barrier = pltpu.get_barrier_semaphore()
    pl.semaphore_signal(barrier, inc=1, device_id=partner, device_id_type=MESH)
    for d in range(1, 8):
        for peer in (z * 8 + (y + d) % 8, (z + d) % 8 * 8 + y):
            pl.semaphore_signal(barrier, inc=1, device_id=(peer, row), device_id_type=MESH)
    pl.semaphore_wait(barrier, 15)

    started = []

    def send(way, peer, a, b, own=False, tag=None):
        at = slot(a, b)
        copy = pltpu.make_async_remote_copy(
            src_ref=x_ref.at[core] if own else g_ref.at[core, at],
            dst_ref=g_ref.at[core, at],
            send_sem=send_sem.at[way, at if tag is None else tag],
            recv_sem=recv_sem.at[core, at],
            device_id=peer,
            device_id_type=MESH,
        )
        copy.start()
        started.append(copy)

    def arrived(half, at):
        pltpu.make_async_remote_copy(
            src_ref=g_ref.at[half, at],
            dst_ref=g_ref.at[half, at],
            send_sem=send_sem.at[0, at],
            recv_sem=recv_sem.at[half, at],
            device_id=partner,
            device_id_type=MESH,
        ).wait_recv()

    for d in (1, 7, 2, 6, 3, 5, 4):
        send(0, (slot(i1 + d, i2), row), i1, i2, True, tag=d)
    send(1, right2, i1, i2, True)
    send(2, left2, i1, i2, True)
    local = [
        pltpu.make_async_copy(x_ref.at[h], g_ref.at[h, grp], own_sem.at[h]) for h in range(2)
    ]
    for copy in local:
        copy.start()

    def tokens_y(d):
        return pltpu.make_async_remote_copy(
            src_ref=o_ref.at[:, (y + d) % 8],
            dst_ref=m_ref.at[y],
            send_sem=tok_send.at[0, d],
            recv_sem=tok_recv.at[0, d],
            device_id=(z * 8 + (y + d) % 8, row),
            device_id_type=MESH,
        )

    def tokens_z(d):
        return pltpu.make_async_remote_copy(
            src_ref=m_ref.at[:, (z + d) % 8],
            dst_ref=t_ref.at[z],
            send_sem=tok_send.at[1, d],
            recv_sem=tok_recv.at[1, d],
            device_id=((z + d) % 8 * 8 + y, row),
            device_id_type=MESH,
        )

    tok_own = pltpu.make_async_copy(o_ref.at[:, y], m_ref.at[y], tok_local.at[0])
    tok_own.start()
    for d in range(1, 8):
        tokens_y(d).start()

    line = [0, -1, 1, -2, 2, -3, 3, -4]
    for off in line[1:]:
        arrived(core, slot(i1 + off + 8, i2))
        send(1, right2, i1 + off + 8, i2)
        send(2, left2, i1 + off + 8, i2)
        send(3, partner, i1 + off + 8, i2)

    for dist in range(1, 5):
        if dist == 2:
            tok_own.wait()
            for d in range(1, 8):
                tokens_y(d).wait()
            tok_own = pltpu.make_async_copy(m_ref.at[:, z], t_ref.at[z], tok_local.at[1])
            tok_own.start()
            for d in range(1, 8):
                tokens_z(d).start()
        for n, off in enumerate(line):
            a = i1 + off + 8
            for sign in (-1, 1):
                if dist == 4 and (n % 2 == 0) != (sign < 0):
                    continue
                b = i2 + sign * dist + 8
                arrived(core, slot(a, b))
                if dist < 3 or (dist == 3 and (n % 2 == 0) == (sign < 0)):
                    send(1 if sign < 0 else 2, right2 if sign < 0 else left2, a, b)
                send(3, partner, a, b)

    for n in range(1, 64):
        arrived(1 - core, (grp + n) % 64)
    for copy in started:
        copy.wait_send()
    for copy in local:
        copy.wait()
    tok_own.wait()
    for d in range(1, 8):
        tokens_z(d).wait()


def exchange(x, outgoing):
    any_spec = pl.BlockSpec(memory_space=pl.ANY)
    vm_spec = pl.BlockSpec(memory_space=pltpu.VMEM)
    block = jax.ShapeDtypeStruct((8, 8, 2, 128), BF16)
    return pl.pallas_call(
        gather_kernel,
        name="exchange",
        out_shape=(jax.ShapeDtypeStruct((2, 64, 8, HALF), BF16), block, block),
        in_specs=[vm_spec, any_spec],
        out_specs=(vm_spec, any_spec, any_spec),
        scratch_shapes=[
            pltpu.SemaphoreType.DMA((2,)),
            pltpu.SemaphoreType.DMA((4, 64)),
            pltpu.SemaphoreType.DMA((2, 64)),
            pltpu.SemaphoreType.DMA((2,)),
            pltpu.SemaphoreType.DMA((2, 8)),
            pltpu.SemaphoreType.DMA((2, 8)),
        ],
        compiler_params=pltpu.CompilerParams(collective_id=0, has_side_effects=True),
    )(x, outgoing)


def pack_weights(w_mid, w_out):
    mid = jnp.pad(w_mid.reshape(6, 3, 9 * C2), ((0, 0), (0, 0), (0, NB - 9 * C2)))
    out = jnp.pad(w_out.reshape(3, 3, 9 * C3), ((0, 0), (0, 0), (0, OB - 9 * C3)))
    none = jnp.zeros((OB,), BF16)
    extra = [out[0, 0], out[0, 1], out[0, 2], out[2, 0], out[2, 2], none]
    extra += [out[1, 0], out[1, 1], out[1, 2], out[2, 1], none, none]
    extra = jnp.concatenate(extra).reshape(2, 3 * NB)
    piece = jnp.concatenate([mid.reshape(6, 3 * NB), extra], axis=0)
    return jnp.stack([piece[:, :HALF], piece[:, HALF:]])


def per_device(latents, frames, offsets, assign, w_in, w_mid, w_out, gain_in, gain_mid, gain_out):
    groups = lax.axis_size("grp")
    row_index = lax.axis_index("row")
    group_index = lax.axis_index("grp")
    channels = w_in.shape[0]
    cap_vals = latents.shape[1] // groups
    cap_tokens = cap_vals // channels
    span_len = cap_tokens // FMAX

    win = w_in.transpose(1, 0, 2).reshape(27 * channels, C1)

    table = latents.reshape(128, 128)
    packed = (offsets * 8 + frames).at[assign].get(mode="promise_in_bounds")
    start = packed // 8
    lasting = packed % 8
    length = lasting * (span_len * channels)
    first = start // 8
    want = first[:, None] + jnp.arange(3, dtype=jnp.int32)[None, :]
    pick = (want.reshape(-1)[:, None] == jnp.arange(128, dtype=jnp.int32)[None, :]).astype(BF16)
    rows = jnp.dot(pick, table, preferred_element_type=F32).astype(BF16).reshape(groups, 384)
    shift = (start % 8)[:, None]
    for bit in (4, 2, 1):
        moved = jnp.pad(rows[:, 16 * bit :], ((0, 0), (0, 16 * bit)))
        rows = jnp.where((shift & bit) != 0, moved, rows)
    keep = jnp.arange(cap_vals, dtype=jnp.int32)[None, :] < length[:, None]
    outgoing = jnp.where(keep, rows[:, :cap_vals], jnp.zeros((), BF16))
    weights, incoming, _ = exchange(pack_weights(w_mid, w_out), outgoing.reshape(8, 8, 2, 128))
    weights = weights.reshape(2, 8 * groups, HALF)

    tokens = incoming.reshape(groups * cap_tokens, channels)
    mine = jnp.arange(groups, dtype=jnp.int32) == group_index
    count = jnp.sum(jnp.where(mine, lasting, 0))
    fill_len = count * span_len
    frame_ids = jnp.arange(FMAX, dtype=jnp.int32)[:, None, None]
    row_ids = row_index * RL - 2 + jnp.arange(6, dtype=jnp.int32)[None, :, None]
    col_ids = jnp.arange(WL, dtype=jnp.int32)[None, None, :]
    position = (frame_ids * 16 + row_ids) * WL + col_ids
    valid = (row_ids >= 0) & (row_ids < 16) & (frame_ids < count) & (col_ids >= 0)
    position = jnp.where(valid, position, 0)
    shard = jnp.minimum(position // fill_len, groups - 1)
    within = position % fill_len
    picked = tokens[(shard * cap_tokens + within).reshape(-1)]
    picked = jnp.where(valid.reshape(-1, 1), picked, jnp.zeros((), BF16))
    xt = jnp.pad(picked.T, ((0, 0), (320, 64)))
    info = jnp.stack([row_index.astype(jnp.int32), count])
    gout = jnp.pad(gain_out, (0, 128 - C3)).reshape(1, 128)
    return decode(
        info, xt, win, weights, gain_in, gain_mid, gout
    )


def solution(mesh):
    placed = (
        P("grp", None),
        P(),
        P(),
        P(),
        P(),
        P("grp", None, None),
        P("grp", None, None),
        P(),
        P(),
        P(),
    )
    return jax.shard_map(
        per_device,
        mesh=mesh,
        in_specs=placed,
        out_specs=P("grp", None, "row", None),
        check_vma=False,
    )
```
